32 devices in a mesh: row: 4 (over x, core), col: 8 (over z, y).
Axes of the slice: x: 2, y: 2, z: 4, core: 2. Of those that a mesh axis runs over, the one named last changes fastest.
Arguments:
- ci_coeffs: float32 [8192, 8192], P('row', 'col'), may hold values from -6 to 6
- h_blocks: float32 [64, 24, 128, 128], P('col'), may hold values from -0.109375 to 0.109375
- block_columns: int32 [64, 24], P('col'), may hold values from 0 to 63, as said below
Outputs:
- sigma: float32 [8192, 8192], P('row', 'col')
The draws below stay inside these ranges and needn't reach their ends.
Inputs may be any that keep to these rules, and one draw needn't show every extreme that they name: `block_columns`: block row J lists 24 different block columns, J itself among them, each of the form (J + t) modulo 64 with -16 <= t < 16.
All inputs are finite; a program needn't handle non-finite values.
Results may differ from the reference program's by a relative error of at most 0.0001.
Values sent between devices are 32-bit elements; how exact they have to be, the bound alone decides.
No kernel may reach another device: no remote copies, remote signals or barrier semaphores. Data moves between devices by JAX's collectives and lax.ppermute only.
A program may use at most 192 MiB of HBM per device.

```python
import jax
import jax.numpy as jnp
from jax import lax

BS = 128
K = 24
HALF = 16
NBLK = 64
N = 8192


def draw_block_columns(key, part):
    breadth = 2 * HALF - 1
    scores = jax.random.randint(key, (NBLK, breadth), 0, 2 ** 20) * breadth + jnp.arange(breadth, dtype=jnp.int32)[None, :]
    ranking = jnp.argsort(scores, axis=1)
    chosen = ranking[:, :K - 1]
    shifted = chosen - HALF + (chosen >= HALF).astype(jnp.int32)
    offsets = jnp.concatenate([jnp.zeros((NBLK, 1), jnp.int32), shifted], axis=1)
    columns = (jnp.arange(NBLK, dtype=jnp.int32)[:, None] + offsets) % NBLK
    return jnp.sort(columns, axis=1).astype(jnp.int32)


def steps_of(key, extent, shards, smallest, high):
    loudness, own = 1.0, jax.random.fold_in(key, 6)
    for dim, parts in shards:
        steps = jnp.exp(jax.random.uniform(jax.random.fold_in(own, dim), (parts,), jnp.float32, smallest / len(shards), high / len(shards)))
        loudness = loudness * jnp.repeat(steps, extent[dim] // parts).reshape([-1 if axis == dim else 1 for axis in range(len(extent))])
    return loudness


def bell_draw(key, shape, spread, bound, shards=(), held_as=jnp.bfloat16):
    entries = jax.random.normal(key, shape, jnp.float32) * spread
    if len(shards) > 0:
        entries = steps_of(key, shape, shards, -0.22, 0.18) * entries
    return jnp.clip(entries, min=-bound, max=bound).astype(held_as)


def setup_inputs(seed: int = 0) -> dict:
    key_of = jax.random.split(jax.random.key(seed), 4)
    return {
        "ci_coeffs": bell_draw(key_of[0], (N, N), 1.0, 6.0, ((0, 4), (1, 8)), jnp.float32),
        "h_blocks": bell_draw(key_of[1], (NBLK, K, BS, BS), (K * BS) ** -0.5, 0.109375, ((0, 8),), jnp.float32),
        "block_columns": draw_block_columns(jax.random.fold_in(key_of[3], 71), 0),
    }


def reference(ci_coeffs, h_blocks, block_columns):
    strings = NBLK * BS
    column_blocks = jnp.transpose(ci_coeffs.reshape(strings, NBLK, BS), (1, 0, 2))

    def accumulate(running, inputs):
        column_block, blocks_row, targets = inputs
        products = jnp.einsum("nb,kbe->kne", column_block, blocks_row, precision=lax.Precision.HIGHEST)
        return running.at[targets].add(products), None

    initial = jnp.zeros((NBLK, strings, BS), jnp.float32)
    gathered, unused = lax.scan(accumulate, initial, (column_blocks, h_blocks, block_columns))
    half_sigma = jnp.transpose(gathered, (1, 0, 2)).reshape(strings, strings)
    return half_sigma + half_sigma.T
```

```python
import functools

import jax
import jax.numpy as jnp
from jax import lax
from jax.experimental import pallas as pl
from jax.experimental.pallas import tpu as pltpu
from jax.sharding import PartitionSpec as P

HALF = 16
AXES = ("row", "col")


def send(block, devices_row, devices_col, target):
    route = []
    for row in range(devices_row):
        for col in range(devices_col):
            to = target(row, col)
            if to is not None:
                route.append((row * devices_col + col, to[0] * devices_col + to[1]))
    return lax.ppermute(block, AXES, route)


def after(block, *others):
    return lax.optimization_barrier((block, *others))[0]


def place_kernel(reach, count, info, columns, blocks, high, low):
    row = pl.program_id(0)
    per_device = pl.num_programs(0)
    size = blocks.shape[-1]
    high[...] = jnp.zeros_like(high)
    low[...] = jnp.zeros_like(low)
    own = info[0] * per_device + row
    for k in range(blocks.shape[1]):
        offset = lax.rem(columns[row, k] - own + count + count // 2, count) - count // 2
        at = pl.multiple_of((row + offset + reach * per_device) * size, size)
        value = blocks[0, k]
        rounded = value.astype(jnp.bfloat16)
        high[:, pl.ds(at, size)] = rounded
        low[:, pl.ds(at, size)] = (value - rounded.astype(jnp.float32)).astype(jnp.bfloat16)


def place_blocks(h_blocks, block_columns, column_index, reach, count):
    per_device, k, size, _ = h_blocks.shape
    width = (2 * reach + 1) * per_device * size
    shape = jax.ShapeDtypeStruct((per_device * size, width), jnp.bfloat16)
    return pl.pallas_call(
        functools.partial(place_kernel, reach, count),
        grid_spec=pltpu.PrefetchScalarGridSpec(
            num_scalar_prefetch=2,
            grid=(per_device,),
            in_specs=[pl.BlockSpec((1, k, size, size), lambda j, *_: (j, 0, 0, 0))],
            out_specs=[pl.BlockSpec((size, width), lambda j, *_: (j, 0))] * 2,
        ),
        out_shape=[shape, shape],
        cost_estimate=pl.CostEstimate(
            flops=0, transcendentals=0, bytes_accessed=h_blocks.size * 4 + shape.size * 4
        ),
        name="place",
    )(jnp.reshape(column_index, (1,)), block_columns, h_blocks)


def product_kernel(where, coeffs, high, low, *rest):
    *addends, out = rest
    value = coeffs[...]
    rounded = value.astype(jnp.bfloat16)
    left = (value - rounded.astype(jnp.float32)).astype(jnp.bfloat16)
    dot = functools.partial(jnp.dot, preferred_element_type=jnp.float32)
    total = dot(rounded, low[...]) + dot(left, high[...])
    total = total + dot(rounded, high[...])
    for addend in addends:
        total = total + addend[...]
    out[...] = total


def product(coeffs, placed, chunk, slot, rows, addends=()):
    depth = coeffs.shape[1]
    tile = min(256, rows)
    tiles = rows // tile
    out_spec = pl.BlockSpec((tile, depth), lambda i, where: (i, 0))
    slot_spec = pl.BlockSpec((depth, depth), lambda i, where: (0, where[1]))
    return pl.pallas_call(
        product_kernel,
        grid_spec=pltpu.PrefetchScalarGridSpec(
            num_scalar_prefetch=1,
            grid=(tiles,),
            in_specs=[
                pl.BlockSpec((tile, depth), lambda i, where: (where[0] * tiles + i, 0)),
                slot_spec,
                slot_spec,
            ]
            + [out_spec] * len(addends),
            out_specs=out_spec,
        ),
        out_shape=jax.ShapeDtypeStruct((rows, depth), jnp.float32),
        cost_estimate=pl.CostEstimate(
            flops=6 * rows * depth * depth,
            transcendentals=0,
            bytes_accessed=4 * rows * depth * (2 + len(addends)) + 4 * depth * depth,
        ),
        name="product",
    )(jnp.stack([chunk, slot]).astype(jnp.int32), coeffs, *placed, *addends)


def finish_kernel(pieces, where, half, *rest):
    mirrored = rest[0][...]
    for piece in rest[1:pieces]:
        mirrored = mirrored + piece[...]
    rest[-1][...] = half[...] + mirrored.T


def finish(half, pieces, chunk, chunks, out=None):
    rows, depth = half.shape
    tile = min(256, rows)
    tiles = rows // tile
    half_spec = pl.BlockSpec((tile, depth), lambda i, where: (i, 0))
    piece_spec = pl.BlockSpec((depth, tile), lambda i, where: (0, i))
    operands = [half, *pieces] + ([] if out is None else [out])
    return pl.pallas_call(
        functools.partial(finish_kernel, len(pieces)),
        grid_spec=pltpu.PrefetchScalarGridSpec(
            num_scalar_prefetch=1,
            grid=(tiles,),
            in_specs=[half_spec]
            + [piece_spec] * len(pieces)
            + ([] if out is None else [pl.BlockSpec(memory_space=pl.ANY)]),
            out_specs=pl.BlockSpec((tile, depth), lambda i, where: (where[0] * tiles + i, 0)),
        ),
        out_shape=jax.ShapeDtypeStruct((chunks * rows, depth), jnp.float32),
        input_output_aliases={} if out is None else {len(operands): 0},
        cost_estimate=pl.CostEstimate(
            flops=rows * depth * (len(pieces) + 1),
            transcendentals=0,
            bytes_accessed=4 * rows * depth * (2 + len(pieces)),
        ),
        name="finish",
    )(jnp.reshape(chunk, (1,)).astype(jnp.int32), *operands)


def local(ci_coeffs, h_blocks, block_columns):
    per_device = h_blocks.shape[0]
    devices_row, devices_col = lax.axis_size("row"), lax.axis_size("col")
    rows = ci_coeffs.shape[1]
    chunks = ci_coeffs.shape[0] // rows
    far = ((HALF + per_device - 1) // per_device + 1) // 2
    reach = 2 * far
    hop = functools.partial(send, devices_row=devices_row, devices_col=devices_col)
    column_index = lax.axis_index("col")
    parity = column_index % 2
    first_chunk = column_index % chunks

    placed = place_blocks(
        h_blocks, block_columns, column_index, reach, per_device * devices_col
    )

    def own(turn, slot, addends=()):
        return product(ci_coeffs, placed, first_chunk ^ turn, reach + slot, rows, addends)

    def for_neighbour(turn, shift):
        chunk = ((column_index ^ 1) % chunks) ^ turn
        return product(ci_coeffs, placed, chunk, reach + 2 * shift + 1 - 2 * parity, rows)

    def to_neighbour(block):
        return hop(block, target=lambda row, col: (row, col ^ 1))

    def along(block, shift_of):
        return hop(
            block, target=lambda row, col: (row, (col + 2 * shift_of(col % 2)) % devices_col)
        )

    outward = lambda p: far if p == 1 else -far
    inward = lambda p: -outward(p)
    outward_here = jnp.where(parity == 1, far, -far)

    halves = []
    last_near, last_outward, last_inward = None, None, None
    for turn in range(chunks):
        edge = own(turn, 2 * outward_here)
        if last_outward is not None:
            edge = after(edge, last_outward)
        last_outward = from_outward = along(edge, outward)

        near = for_neighbour(turn, outward_here)
        if last_near is not None:
            near = after(near, last_near)
        near = to_neighbour(near)
        edge = own(turn, -2 * outward_here)
        edge = edge + near
        if last_inward is not None:
            edge = after(edge, last_inward)
        last_inward = from_inward = along(edge, inward)

        total = []
        for shift in range(1 - far, far):
            step = to_neighbour(after(for_neighbour(turn, shift), near))
            near = step
            if shift != 0:
                moved = own(turn, 2 * shift, (step,))
                step = along(moved, lambda p, shift=shift: shift)
            total.append(step)
        last_near = near
        half = own(turn, 0, (from_outward, *total))
        halves.append(half + from_inward)

    part = devices_row // 2

    def mirror_of(turn):
        def target(row, col):
            return col // chunks, chunks * row + ((col % chunks) ^ turn)

        return target

    def crossing(row, col):
        return row // part != (col // chunks) // part

    def over(row):
        return (row + part) % devices_row

    out = None
    for turn, half in enumerate(halves):
        target = mirror_of(turn)
        if turn % 2 == 0 and turn + 1 < chunks:
            direct = hop(
                half,
                target=lambda row, col: None if crossing(row, col) else target(row, col),
            )
            moved = hop(
                half, target=lambda row, col: (over(row), col) if crossing(row, col) else None
            )
            moved = after(moved, halves[turn + 1])
            moved = hop(
                moved,
                target=lambda row, col: target(over(row), col)
                if crossing(over(row), col)
                else None,
            )
            pieces = (direct, moved)
        else:
            pieces = (hop(half, target=target),)
        out = finish(half, pieces, first_chunk ^ turn, chunks, out)
    return out


def solution(mesh):
    return jax.shard_map(
        local,
        mesh=mesh,
        in_specs=(P("row", "col"), P("col", None, None, None), P("col", None)),
        out_specs=P("row", "col"),
        check_vma=False,
    )
```
